32 devices in a mesh: prompt: 8 (over y, x, core), seq: 4 (over z).
Axes of the slice: x: 2, y: 2, z: 4, core: 2. Of those that a mesh axis runs over, the one named last changes fastest.
Arguments:
- queries: bfloat16 [8, 512, 4096], P('prompt', 'seq'), may hold values from -8 to 8
- self_keys: bfloat16 [8, 512, 4096], P('prompt', 'seq'), may hold values from -8 to 8
- self_values: bfloat16 [8, 512, 4096], P('prompt', 'seq'), may hold values from -6 to 6
- cross_queries: bfloat16 [8, 512, 4096], P('prompt', 'seq')
- context: bfloat16 [8, 512, 5120], P('prompt', 'seq')
- key_weight: bfloat16 [5120, 4096], P('prompt', 'seq')
- value_weight: bfloat16 [5120, 4096], P('prompt', 'seq'), may hold values from -0.078125 to 0.078125
- lengths: int32 [8], P('prompt'), may hold values from 64 to 512, as said below
Outputs:
- attended: bfloat16 [8, 512, 4096], P('prompt', 'seq')
The draws below stay inside these ranges and needn't reach their ends.
Inputs may be any that keep to these rules, and one draw needn't show every extreme that they name: `lengths`: each prompt's number of text tokens; some prompt has all 512.
All inputs are finite; a program needn't handle non-finite values.
Results may differ from the reference program's by a relative error of at most 0.007.
Values may be sent and summed in bfloat16 or wider, within the bound.
A program may use at most 128 MiB of HBM per device.

```python
import math
import jax
import jax.numpy as jnp
from jax import lax

D = 5120
HD = 128
HEADS = 32
TXT = 512
PROMPTS = 8
SEQ_LEN = 512
HW = 4096


def self_pair(key):
    query_seed, key_seed = jax.random.split(jax.random.fold_in(key, 7), 2)
    full_shape = (PROMPTS, SEQ_LEN, HEADS * HD)
    query_draw = jnp.clip(jax.random.normal(query_seed, full_shape, jnp.float32), -6.0, 6.0)
    key_draw = jnp.clip(jax.random.normal(key_seed, full_shape, jnp.float32), -6.0, 6.0)
    return (query_draw, key_draw)


def cross_parts(key):
    weight_seed, context_seed, query_seed = jax.random.split(jax.random.fold_in(key, 13), 3)
    weight_draw = jax.random.normal(weight_seed, (D, HEADS * HD), jnp.float32) / math.sqrt(D)
    context_draw = jnp.clip(jax.random.normal(context_seed, (PROMPTS, TXT, D), jnp.float32), -6.0, 6.0)
    query_draw = jnp.clip(jax.random.normal(query_seed, (PROMPTS, SEQ_LEN, HEADS * HD), jnp.float32), -6.0, 6.0)
    return (weight_draw, context_draw, query_draw)


def draw_queries(key, part):
    return self_pair(key)[0].astype(jnp.bfloat16)


def draw_self_keys(key, part):
    return self_pair(key)[1].astype(jnp.bfloat16)


def draw_key_weight(key, part):
    return cross_parts(key)[0].astype(jnp.bfloat16)


def draw_context(key, part):
    return cross_parts(key)[1].astype(jnp.bfloat16)


def draw_cross_queries(key, part):
    return cross_parts(key)[2].astype(jnp.bfloat16)


def draw_lengths(key, part):
    first_seed, second_seed, longest_seed = jax.random.split(jax.random.fold_in(key, 29), 3)
    first_draw = jax.random.randint(first_seed, (PROMPTS,), TXT // 8, TXT + 1)
    second_draw = jax.random.randint(second_seed, (PROMPTS,), TXT // 8, TXT + 1)
    shorter = jnp.minimum(first_draw, second_draw)
    longest = jax.random.randint(longest_seed, (), 0, PROMPTS)
    return jnp.where(jnp.arange(PROMPTS) == longest, TXT, shorter).astype(jnp.int32)


def steps_of(rng, dims, cuts, smallest, high):
    gain, own = 1.0, jax.random.fold_in(rng, 6)
    for axis_at, blocks in cuts:
        draws = jnp.exp(jax.random.uniform(jax.random.fold_in(own, axis_at), (blocks,), jnp.float32, smallest / len(cuts), high / len(cuts)))
        gain = gain * jnp.repeat(draws, dims[axis_at] // blocks).reshape([-1 if axis == axis_at else 1 for axis in range(len(dims))])
    return gain


def gaussian(stream_key, dims, scale, bound, shards=(), kind=jnp.bfloat16):
    values = scale * jax.random.normal(stream_key, dims, jnp.float32)
    if shards:
        values = values * steps_of(stream_key, dims, shards, -0.22, 0.18)
    return jnp.clip(values, -bound, bound).astype(kind)


def setup_inputs(seed: int = 0) -> dict:
    splits = jax.random.split(jax.random.key(seed), 9)
    return {
        "queries": draw_queries(jax.random.fold_in(splits[8], 71), 0),
        "self_keys": draw_self_keys(jax.random.fold_in(splits[8], 71), 0),
        "self_values": gaussian(splits[2], (PROMPTS, SEQ_LEN, HW), 1.0, 6.0, ((0, 8), (1, 4))),
        "cross_queries": draw_cross_queries(jax.random.fold_in(splits[8], 71), 0),
        "context": draw_context(jax.random.fold_in(splits[8], 71), 0),
        "key_weight": draw_key_weight(jax.random.fold_in(splits[8], 71), 0),
        "value_weight": gaussian(splits[6], (D, HW), D ** -0.5, 0.078125, ((0, 8), (1, 4))),
        "lengths": draw_lengths(jax.random.fold_in(splits[8], 71), 0),
    }


def attend_head(query_rows, key_rows, value_rows, usable):
    scaling = 1.0 / math.sqrt(HD)
    scores = jnp.dot(query_rows, key_rows.T, preferred_element_type=jnp.float32) * scaling
    row_max = lax.optimization_barrier(jnp.max(jnp.where(usable[None, :], scores, -jnp.inf), axis=1))
    shifted = jnp.where(usable[None, :], scores, row_max[:, None]) - row_max[:, None]
    weights = jnp.where(usable[None, :], jnp.exp(shifted), jnp.zeros_like(shifted))
    totals = lax.optimization_barrier(jnp.sum(weights, axis=1))
    mixed = jnp.dot(weights.astype(jnp.bfloat16), value_rows, preferred_element_type=jnp.float32)
    return (mixed / totals[:, None]).astype(jnp.bfloat16)

def by_head(matrix):
    return matrix.reshape(matrix.shape[0], HEADS, HD).transpose(1, 0, 2)

def reference(queries, self_keys, self_values, cross_queries, context, key_weight, value_weight, lengths):

    def one_prompt(inputs):
        query_all, key_all, value_all, cross_all, context_rows, length = inputs
        text_keys = jnp.dot(context_rows, key_weight, preferred_element_type=jnp.float32).astype(jnp.bfloat16)
        text_values = jnp.dot(context_rows, value_weight, preferred_element_type=jnp.float32).astype(jnp.bfloat16)
        every_token = jnp.ones((SEQ_LEN,), dtype=bool)
        text_usable = jnp.arange(TXT, dtype=jnp.int32) < length

        def one_head(parts):
            query_head, key_head, value_head, cross_head, text_key_head, text_value_head = parts
            self_part = attend_head(query_head, key_head, value_head, every_token)
            cross_part = attend_head(cross_head, text_key_head, text_value_head, text_usable)
            return (self_part.astype(jnp.float32) + cross_part.astype(jnp.float32)).astype(jnp.bfloat16)
        mixed = lax.map(one_head, (by_head(query_all), by_head(key_all), by_head(value_all), by_head(cross_all), by_head(text_keys), by_head(text_values)))
        return mixed.transpose(1, 0, 2).reshape(SEQ_LEN, HEADS * HD)
    return lax.map(one_prompt, (queries, self_keys, self_values, cross_queries, context, lengths))
```

```python
import functools
import math

import jax
import jax.numpy as jnp
from jax import lax
from jax.experimental import pallas as pl
from jax.experimental.pallas import tpu as pltpu
from jax.sharding import PartitionSpec as P

HD = 128
CORES = 2
Q, K, V, CTX, CQ = range(5)


def kernel(
    seq_size,
    prompt_size,
    length_ref,
    q_hbm,
    k_hbm,
    v_hbm,
    cq_hbm,
    ctx_hbm,
    wk_hbm,
    wv_hbm,
    out_hbm,
    q_buf,
    k_buf,
    v_buf,
    cq_buf,
    ctx_buf,
    wk_buf,
    wv_buf,
    text_keys,
    text_values,
    self_buf,
    out_buf,
    local_sem,
    seq_send,
    seq_recv,
    chip_send,
    chip_recv,
    pair_send,
    pair_recv,
    out_send,
    out_recv,
):
    seq = lax.axis_index("seq")
    prompt = lax.axis_index("prompt")
    chips = prompt_size // CORES
    chip = prompt // CORES
    core = prompt % CORES
    partner = chip * CORES + (1 - core)
    tokens = q_hbm.shape[0]
    width = wk_hbm.shape[1]
    depth = wk_hbm.shape[0]
    heads = width // HD
    scaling = 1.0 / math.sqrt(HD)

    def seq_peer(offset):
        return lax.rem(seq + offset, seq_size)

    def seq_source(offset):
        return lax.rem(seq + seq_size - offset, seq_size)

    def chip_peer(offset):
        return lax.rem(chip + offset, chips) * CORES + core

    def chip_source(offset):
        return lax.rem(chip + chips - offset, chips) * CORES + core

    barrier = pltpu.get_barrier_semaphore()
    for offset in range(1, seq_size):
        pl.semaphore_signal(
            barrier, inc=1, device_id={"seq": seq_peer(offset)}, device_id_type=pl.DeviceIdType.MESH
        )
    for offset in range(1, chips):
        pl.semaphore_signal(
            barrier,
            inc=1,
            device_id={"prompt": chip_peer(offset)},
            device_id_type=pl.DeviceIdType.MESH,
        )
    pl.semaphore_signal(
        barrier, inc=1, device_id={"prompt": partner}, device_id_type=pl.DeviceIdType.MESH
    )
    pl.semaphore_wait(barrier, seq_size - 1 + chips - 1 + 1)

    def token_rows(owner):
        return pl.ds(pl.multiple_of(owner * tokens, tokens), tokens)

    def text_rows(owner):
        text = ctx_hbm.shape[0]
        return pl.ds(pl.multiple_of(owner * text, text), text)

    def head_columns(owner):
        return pl.ds(pl.multiple_of(owner * width, width), width)

    def weight_rows(owner):
        return pl.ds(pl.multiple_of(owner * depth, depth), depth)

    sources = {Q: q_hbm, K: k_hbm, V: v_hbm, CTX: ctx_hbm, CQ: cq_hbm}
    buffers = {Q: q_buf, K: k_buf, V: v_buf, CTX: ctx_buf, CQ: cq_buf}

    def piece(which, owner):
        if which == CTX:
            return sources[which]
        return sources[which].at[:, head_columns(owner)]

    def landing(which, owner):
        rows = text_rows(owner) if which == CTX else token_rows(owner)
        return buffers[which].at[rows]

    def seq_copy(which, offset):
        return pltpu.make_async_remote_copy(
            src_ref=piece(which, seq_peer(offset)),
            dst_ref=landing(which, seq),
            send_sem=seq_send.at[which, offset],
            recv_sem=seq_recv.at[which, offset],
            device_id={"seq": seq_peer(offset)},
            device_id_type=pl.DeviceIdType.MESH,
        )

    weights = ((wk_hbm, wk_buf), (wv_hbm, wv_buf))

    def chip_copy(which, offset):
        shard, gathered = weights[which]
        return pltpu.make_async_remote_copy(
            src_ref=shard,
            dst_ref=gathered.at[weight_rows(prompt)],
            send_sem=chip_send.at[which, offset],
            recv_sem=chip_recv.at[which, offset],
            device_id={"prompt": chip_peer(offset)},
            device_id_type=pl.DeviceIdType.MESH,
        )

    def pair_copy(which, offset):
        shard, gathered = weights[which]
        rows = weight_rows(chip_source(offset))
        return pltpu.make_async_remote_copy(
            src_ref=shard if offset == 0 else gathered.at[rows],
            dst_ref=gathered.at[rows],
            send_sem=pair_send.at[which, offset],
            recv_sem=pair_recv.at[which, offset],
            device_id={"prompt": partner},
            device_id_type=pl.DeviceIdType.MESH,
        )

    def out_copy(offset):
        return pltpu.make_async_remote_copy(
            src_ref=out_buf.at[token_rows(seq_source(offset))],
            dst_ref=out_hbm.at[:, head_columns(seq)],
            send_sem=out_send.at[offset],
            recv_sem=out_recv.at[offset],
            device_id={"seq": seq_source(offset)},
            device_id_type=pl.DeviceIdType.MESH,
        )

    offsets = range(1, seq_size)
    for which in (Q, K, V):
        for offset in offsets:
            seq_copy(which, offset).start()
    for which in range(2):
        for offset in range(1, chips):
            chip_copy(which, offset).start()
    for which in (CTX, CQ):
        for offset in offsets:
            seq_copy(which, offset).start()
    local_copies = [
        pltpu.make_async_copy(
            piece(which, seq), landing(which, seq), local_sem.at[which]
        )
        for which in (Q, K, V, CTX, CQ)
    ] + [
        pltpu.make_async_copy(
            weights[which][0], weights[which][1].at[weight_rows(prompt)], local_sem.at[5 + which]
        )
        for which in range(2)
    ]
    for copy in local_copies:
        copy.start()
    for which in range(2):
        pair_copy(which, 0).start()
    for copy in local_copies:
        copy.wait()

    def head_attend(query, key, value, length):
        scores = lax.dot_general(
            query, key, (((1,), (1,)), ((), ())), preferred_element_type=jnp.float32
        )
        if length is not None:
            slot = lax.broadcasted_iota(jnp.int32, scores.shape, 1)
            scores = jnp.where(slot < length, scores, -jnp.inf)
        row_max = jnp.max(scores, axis=1, keepdims=True)
        exps = jnp.exp((scores - row_max) * scaling)
        totals = jnp.sum(exps, axis=1, keepdims=True)
        mixed = jnp.dot(exps.astype(jnp.bfloat16), value, preferred_element_type=jnp.float32)
        return (mixed / totals).astype(jnp.bfloat16)

    def forward(which):
        for offset in range(1, chips):
            chip_copy(which, offset).wait_recv()
            pair_copy(which, offset).start()

    forward(0)
    for which in (Q, K, V):
        for offset in offsets:
            seq_copy(which, offset).wait_recv()

    def self_head(head, carry):
        columns = pl.ds(pl.multiple_of(head * HD, HD), HD)
        key = k_buf[:, columns]
        value = v_buf[:, columns]

        def block(index, inner):
            rows = token_rows(index)
            self_buf[rows, columns] = head_attend(q_buf[rows, columns], key, value, None)
            return inner

        return lax.fori_loop(0, seq_size, block, carry)

    lax.fori_loop(0, heads, self_head, 0)

    forward(1)
    for offset in offsets:
        seq_copy(CTX, offset).wait_recv()

    def project(which, target):
        for offset in range(chips):
            pair_copy(which, offset).wait_recv()
        gathered = weights[which][1]
        tile = math.gcd(width, 256)

        def column_tile(index, carry):
            columns = pl.ds(pl.multiple_of(index * tile, tile), tile)
            target[:, columns] = jnp.dot(
                ctx_buf[...], gathered[:, columns], preferred_element_type=jnp.float32
            ).astype(jnp.bfloat16)
            return carry

        lax.fori_loop(0, width // tile, column_tile, 0)

    project(0, text_keys)
    project(1, text_values)
    length = length_ref[0]

    for offset in tuple(offsets) + (0,):
        if offset:
            seq_copy(CQ, offset).wait_recv()
        rows = token_rows(seq_source(offset))

        def cross_head(head, carry):
            columns = pl.ds(pl.multiple_of(head * HD, HD), HD)
            part = head_attend(
                cq_buf[rows, columns], text_keys[:, columns], text_values[:, columns], length
            )
            out_buf[rows, columns] = (
                self_buf[rows, columns].astype(jnp.float32) + part.astype(jnp.float32)
            ).astype(jnp.bfloat16)
            return carry

        lax.fori_loop(0, heads, cross_head, 0)
        if offset:
            out_copy(offset).start()
    own = pltpu.make_async_copy(
        out_buf.at[token_rows(seq)], out_hbm.at[:, head_columns(seq)], local_sem.at[7]
    )
    own.start()

    for which in (Q, K, V, CTX, CQ):
        for offset in offsets:
            seq_copy(which, offset).wait_send()
    for which in range(2):
        for offset in range(1, chips):
            chip_copy(which, offset).wait_send()
        for offset in range(chips):
            pair_copy(which, offset).wait_send()
    own.wait()
    for offset in offsets:
        out_copy(offset).wait()


def body(
    seq_size,
    prompt_size,
    queries,
    self_keys,
    self_values,
    cross_queries,
    context,
    key_weight,
    value_weight,
    lengths,
):
    tokens = queries.shape[1]
    full = tokens * seq_size
    width = key_weight.shape[1]
    model = context.shape[2]
    chips = prompt_size // CORES
    text_full = context.shape[1] * seq_size
    activations = pltpu.VMEM((full, width), jnp.bfloat16)
    texts = pltpu.VMEM((text_full, width), jnp.bfloat16)
    dma = pltpu.SemaphoreType.DMA
    attended = pl.pallas_call(
        functools.partial(kernel, seq_size, prompt_size),
        out_shape=jax.ShapeDtypeStruct(queries.shape[1:], jnp.bfloat16),
        in_specs=[pl.BlockSpec(memory_space=pltpu.SMEM)]
        + [pl.BlockSpec(memory_space=pl.ANY)] * 7,
        out_specs=pl.BlockSpec(memory_space=pl.ANY),
        scratch_shapes=[activations] * 4
        + [pltpu.VMEM((text_full, model), jnp.bfloat16)]
        + [pltpu.VMEM((model, width), jnp.bfloat16)] * 2
        + [texts] * 2
        + [activations] * 2
        + [
            dma((8,)),
            dma((5, seq_size)),
            dma((5, seq_size)),
            dma((2, chips)),
            dma((2, chips)),
            dma((2, chips)),
            dma((2, chips)),
            dma((seq_size,)),
            dma((seq_size,)),
        ],
        compiler_params=pltpu.CompilerParams(
            collective_id=0, has_side_effects=True, vmem_limit_bytes=60 * 1024 * 1024
        ),
    )(
        lengths,
        queries[0],
        self_keys[0],
        self_values[0],
        cross_queries[0],
        context[0],
        key_weight,
        value_weight,
    )
    return attended[None]


def solution(mesh):
    in_specs = (
        P("prompt", "seq", None),
        P("prompt", "seq", None),
        P("prompt", "seq", None),
        P("prompt", "seq", None),
        P("prompt", "seq", None),
        P("prompt", "seq"),
        P("prompt", "seq"),
        P("prompt"),
    )
    out_specs = P("prompt", "seq", None)
    step = functools.partial(body, mesh.shape["seq"], mesh.shape["prompt"])
    return jax.shard_map(step, mesh=mesh, in_specs=in_specs, out_specs=out_specs, check_vma=False)
```

```python
import functools
import math

import jax
import jax.numpy as jnp
from jax import lax
from jax.experimental import pallas as pl
from jax.experimental.pallas import tpu as pltpu
from jax.sharding import PartitionSpec as P

HD = 128
CORES = 2
Q, K, V, CTX, CQ = range(5)


def kernel(
    seq_size,
    prompt_size,
    length_ref,
    q_hbm,
    k_hbm,
    v_hbm,
    cq_hbm,
    ctx_hbm,
    wk_hbm,
    wv_hbm,
    out_hbm,
    q_buf,
    k_buf,
    v_buf,
    cq_buf,
    ctx_buf,
    wk_buf,
    wv_buf,
    text_keys,
    text_values,
    out_buf,
    local_sem,
    seq_send,
    seq_recv,
    text_send,
    text_recv,
    chip_send,
    chip_recv,
    pair_send,
    pair_recv,
    out_send,
    out_recv,
):
    seq = lax.axis_index("seq")
    prompt = lax.axis_index("prompt")
    chips = prompt_size // CORES
    chip = prompt // CORES
    core = prompt % CORES
    partner = chip * CORES + (1 - core)
    tokens = q_hbm.shape[0]
    width = wk_hbm.shape[1]
    depth = wk_hbm.shape[0]
    heads = width // HD
    scaling = 1.0 / math.sqrt(HD)

    def seq_peer(offset):
        return lax.rem(seq + offset, seq_size)

    def seq_source(offset):
        return lax.rem(seq + seq_size - offset, seq_size)

    def chip_peer(offset):
        return lax.rem(chip + offset, chips) * CORES + core

    def chip_source(offset):
        return lax.rem(chip + chips - offset, chips) * CORES + core

    barrier = pltpu.get_barrier_semaphore()
    for offset in range(1, seq_size):
        pl.semaphore_signal(
            barrier, inc=1, device_id={"seq": seq_peer(offset)}, device_id_type=pl.DeviceIdType.MESH
        )
    for offset in range(1, chips):
        pl.semaphore_signal(
            barrier,
            inc=1,
            device_id={"prompt": chip_peer(offset)},
            device_id_type=pl.DeviceIdType.MESH,
        )
    pl.semaphore_signal(
        barrier, inc=1, device_id={"prompt": partner}, device_id_type=pl.DeviceIdType.MESH
    )
    pl.semaphore_wait(barrier, seq_size - 1 + chips - 1 + 1)

    def token_rows(owner):
        return pl.ds(pl.multiple_of(owner * tokens, tokens), tokens)

    def text_rows(owner):
        text = ctx_hbm.shape[0]
        return pl.ds(pl.multiple_of(owner * text, text), text)

    def head_columns(owner):
        return pl.ds(pl.multiple_of(owner * width, width), width)

    def weight_rows(owner):
        return pl.ds(pl.multiple_of(owner * depth, depth), depth)

    sources = {Q: q_hbm, K: k_hbm, V: v_hbm, CTX: ctx_hbm, CQ: cq_hbm}
    buffers = {Q: q_buf, K: k_buf, V: v_buf, CTX: ctx_buf, CQ: cq_buf}

    def piece(which, owner):
        if which == CTX:
            return sources[which]
        return sources[which].at[:, head_columns(owner)]

    def landing(which, owner):
        rows = text_rows(owner) if which == CTX else token_rows(owner)
        return buffers[which].at[rows]

    def seq_copy(which, offset):
        return pltpu.make_async_remote_copy(
            src_ref=piece(which, seq_peer(offset)),
            dst_ref=landing(which, seq),
            send_sem=seq_send.at[which, offset],
            recv_sem=seq_recv.at[which, offset],
            device_id={"seq": seq_peer(offset)},
            device_id_type=pl.DeviceIdType.MESH,
        )

    def text_start_here(way, hop):
        if way == 0:
            return (seq >= hop) & (seq + 1 < seq_size)
        return (seq + hop < seq_size) & (seq >= 1)

    def text_lands_here(way, hop):
        return seq >= hop + 1 if way == 0 else seq + 1 + hop < seq_size

    def text_copy(way, hop):
        owner = seq - hop if way == 0 else seq + hop
        peer = seq_peer(1 if way == 0 else seq_size - 1)
        rows = text_rows(owner)
        return pltpu.make_async_remote_copy(
            src_ref=ctx_hbm if hop == 0 else ctx_buf.at[rows],
            dst_ref=ctx_buf.at[rows],
            send_sem=text_send.at[way, hop],
            recv_sem=text_recv.at[way, hop],
            device_id={"seq": peer},
            device_id_type=pl.DeviceIdType.MESH,
        )

    def start_text(hop):
        for way in range(2):

            @pl.when(text_start_here(way, hop))
            def _():
                text_copy(way, hop).start()

    def wait_text(hop):
        for way in range(2):

            @pl.when(text_lands_here(way, hop))
            def _():
                text_copy(way, hop).wait_recv()

    weights = ((wk_hbm, wk_buf), (wv_hbm, wv_buf))

    def chip_copy(which, offset):
        shard, gathered = weights[which]
        return pltpu.make_async_remote_copy(
            src_ref=shard,
            dst_ref=gathered.at[weight_rows(prompt)],
            send_sem=chip_send.at[which, offset],
            recv_sem=chip_recv.at[which, offset],
            device_id={"prompt": chip_peer(offset)},
            device_id_type=pl.DeviceIdType.MESH,
        )

    def pair_copy(which, offset):
        shard, gathered = weights[which]
        rows = weight_rows(chip_source(offset))
        return pltpu.make_async_remote_copy(
            src_ref=shard if offset == 0 else gathered.at[rows],
            dst_ref=gathered.at[rows],
            send_sem=pair_send.at[which, offset],
            recv_sem=pair_recv.at[which, offset],
            device_id={"prompt": partner},
            device_id_type=pl.DeviceIdType.MESH,
        )

    def out_copy(offset):
        return pltpu.make_async_remote_copy(
            src_ref=out_buf.at[token_rows(seq_source(offset))],
            dst_ref=out_hbm.at[:, head_columns(seq)],
            send_sem=out_send.at[offset],
            recv_sem=out_recv.at[offset],
            device_id={"seq": seq_source(offset)},
            device_id_type=pl.DeviceIdType.MESH,
        )

    offsets = range(1, seq_size)

    def start_pieces(*group):
        for offset in offsets:
            for which in group:
                seq_copy(which, offset).start()

    groups = [(K,), (V,), (Q, CQ)]
    start_text(0)
    start_pieces(*groups[0])
    for which in range(2):
        for offset in range(1, chips):
            chip_copy(which, offset).start()
    local_copies = [
        pltpu.make_async_copy(
            piece(which, seq), landing(which, seq), local_sem.at[which]
        )
        for which in (Q, K, V, CTX, CQ)
    ] + [
        pltpu.make_async_copy(
            weights[which][0], weights[which][1].at[weight_rows(prompt)], local_sem.at[5 + which]
        )
        for which in range(2)
    ]
    for copy in local_copies:
        copy.start()
    for which in range(2):
        pair_copy(which, 0).start()
    for copy in local_copies:
        copy.wait()

    def head_attend(query, key, value, length):
        scores = lax.dot_general(
            query, key, (((1,), (1,)), ((), ())), preferred_element_type=jnp.float32
        )
        if length is not None:
            slot = lax.broadcasted_iota(jnp.int32, scores.shape, 1)
            scores = jnp.where(slot < length, scores, -jnp.inf)
        row_max = jnp.max(scores, axis=1, keepdims=True)
        exps = jnp.exp((scores - row_max) * scaling)
        totals = jnp.sum(exps, axis=1, keepdims=True)
        mixed = jnp.dot(exps.astype(jnp.bfloat16), value, preferred_element_type=jnp.float32)
        return (mixed / totals).astype(jnp.bfloat16)

    def forward(which):
        for offset in range(1, chips):
            chip_copy(which, offset).wait_recv()
            pair_copy(which, offset).start()

    hops = seq_size - 1
    for hop in range(hops):
        wait_text(hop)
        if hop + 1 < hops:
            start_text(hop + 1)
        if hop + 1 < len(groups):
            start_pieces(*groups[hop + 1])
        if hop == 0:
            forward(0)
    for group in groups[max(hops, 1) :]:
        start_pieces(*group)

    def project(which, target):
        for offset in range(chips):
            pair_copy(which, offset).wait_recv()
        gathered = weights[which][1]
        tile = math.gcd(width, 256)

        def column_tile(index, carry):
            columns = pl.ds(pl.multiple_of(index * tile, tile), tile)
            target[:, columns] = jnp.dot(
                ctx_buf[...], gathered[:, columns], preferred_element_type=jnp.float32
            ).astype(jnp.bfloat16)
            return carry

        lax.fori_loop(0, width // tile, column_tile, 0)

    project(0, text_keys)
    forward(1)
    project(1, text_values)
    for which in (K, V):
        for offset in offsets:
            seq_copy(which, offset).wait_recv()
    length = length_ref[0]

    for offset in range(seq_size):
        if offset:
            seq_copy(Q, offset).wait_recv()
            seq_copy(CQ, offset).wait_recv()
        rows = token_rows(seq_source(offset))

        def head_block(head, carry):
            columns = pl.ds(pl.multiple_of(head * HD, HD), HD)
            alone = head_attend(q_buf[rows, columns], k_buf[:, columns], v_buf[:, columns], None)
            part = head_attend(
                cq_buf[rows, columns], text_keys[:, columns], text_values[:, columns], length
            )
            out_buf[rows, columns] = (
                alone.astype(jnp.float32) + part.astype(jnp.float32)
            ).astype(jnp.bfloat16)
            return carry

        lax.fori_loop(0, heads, head_block, 0)
        if offset:
            out_copy(offset).start()
    own = pltpu.make_async_copy(
        out_buf.at[token_rows(seq)], out_hbm.at[:, head_columns(seq)], local_sem.at[7]
    )
    own.start()

    for which in (Q, K, V, CQ):
        for offset in offsets:
            seq_copy(which, offset).wait_send()
    for hop in range(hops):
        for way in range(2):

            @pl.when(text_start_here(way, hop))
            def _():
                text_copy(way, hop).wait_send()

    for which in range(2):
        for offset in range(1, chips):
            chip_copy(which, offset).wait_send()
        for offset in range(chips):
            pair_copy(which, offset).wait_send()
    own.wait()
    for offset in offsets:
        out_copy(offset).wait()


def body(
    seq_size,
    prompt_size,
    queries,
    self_keys,
    self_values,
    cross_queries,
    context,
    key_weight,
    value_weight,
    lengths,
):
    tokens = queries.shape[1]
    full = tokens * seq_size
    width = key_weight.shape[1]
    model = context.shape[2]
    chips = prompt_size // CORES
    text_full = context.shape[1] * seq_size
    activations = pltpu.VMEM((full, width), jnp.bfloat16)
    texts = pltpu.VMEM((text_full, width), jnp.bfloat16)
    dma = pltpu.SemaphoreType.DMA
    attended = pl.pallas_call(
        functools.partial(kernel, seq_size, prompt_size),
        out_shape=jax.ShapeDtypeStruct(queries.shape[1:], jnp.bfloat16),
        in_specs=[pl.BlockSpec(memory_space=pltpu.SMEM)]
        + [pl.BlockSpec(memory_space=pl.ANY)] * 7,
        out_specs=pl.BlockSpec(memory_space=pl.ANY),
        scratch_shapes=[activations] * 4
        + [pltpu.VMEM((text_full, model), jnp.bfloat16)]
        + [pltpu.VMEM((model, width), jnp.bfloat16)] * 2
        + [texts] * 2
        + [activations]
        + [
            dma((8,)),
            dma((5, seq_size)),
            dma((5, seq_size)),
            dma((2, seq_size)),
            dma((2, seq_size)),
            dma((2, chips)),
            dma((2, chips)),
            dma((2, chips)),
            dma((2, chips)),
            dma((seq_size,)),
            dma((seq_size,)),
        ],
        compiler_params=pltpu.CompilerParams(
            collective_id=0, has_side_effects=True, vmem_limit_bytes=60 * 1024 * 1024
        ),
    )(
        lengths,
        queries[0],
        self_keys[0],
        self_values[0],
        cross_queries[0],
        context[0],
        key_weight,
        value_weight,
    )
    return attended[None]


def solution(mesh):
    in_specs = (
        P("prompt", "seq", None),
        P("prompt", "seq", None),
        P("prompt", "seq", None),
        P("prompt", "seq", None),
        P("prompt", "seq", None),
        P("prompt", "seq"),
        P("prompt", "seq"),
        P("prompt"),
    )
    out_specs = P("prompt", "seq", None)
    step = functools.partial(body, mesh.shape["seq"], mesh.shape["prompt"])
    return jax.shard_map(step, mesh=mesh, in_specs=in_specs, out_specs=out_specs, check_vma=False)
```

```python
import functools
import math

import jax
import jax.numpy as jnp
from jax import lax
from jax.experimental import pallas as pl
from jax.experimental.pallas import tpu as pltpu
from jax.sharding import PartitionSpec as P

HD = 128
CORES = 2
Q, K, V, CTX, CQ = range(5)


def kernel(
    seq_size,
    prompt_size,
    length_ref,
    q_hbm,
    k_hbm,
    v_hbm,
    cq_hbm,
    ctx_hbm,
    wk_hbm,
    wv_hbm,
    out_hbm,
    q_buf,
    k_buf,
    v_buf,
    cq_buf,
    ctx_buf,
    wk_buf,
    wv_buf,
    text_keys,
    text_values,
    out_buf,
    local_sem,
    seq_send,
    seq_recv,
    text_send,
    text_recv,
    chip_send,
    chip_recv,
    pair_send,
    pair_recv,
    out_send,
    out_recv,
):
    seq = lax.axis_index("seq")
    prompt = lax.axis_index("prompt")
    chips = prompt_size // CORES
    chip = prompt // CORES
    core = prompt % CORES
    partner = chip * CORES + (1 - core)
    tokens = q_hbm.shape[0]
    width = wk_hbm.shape[1]
    depth = wk_hbm.shape[0]
    heads = width // HD
    scaling = 1.0 / math.sqrt(HD)

    def seq_peer(offset):
        return lax.rem(seq + offset, seq_size)

    def seq_source(offset):
        return lax.rem(seq + seq_size - offset, seq_size)

    def chip_peer(offset):
        return lax.rem(chip + offset, chips) * CORES + core

    def chip_source(offset):
        return lax.rem(chip + chips - offset, chips) * CORES + core

    barrier = pltpu.get_barrier_semaphore()
    for offset in range(1, seq_size):
        pl.semaphore_signal(
            barrier, inc=1, device_id={"seq": seq_peer(offset)}, device_id_type=pl.DeviceIdType.MESH
        )
    for offset in range(1, chips):
        pl.semaphore_signal(
            barrier,
            inc=1,
            device_id={"prompt": chip_peer(offset)},
            device_id_type=pl.DeviceIdType.MESH,
        )
    pl.semaphore_signal(
        barrier, inc=1, device_id={"prompt": partner}, device_id_type=pl.DeviceIdType.MESH
    )
    pl.semaphore_wait(barrier, seq_size - 1 + chips - 1 + 1)

    def token_rows(owner):
        return pl.ds(pl.multiple_of(owner * tokens, tokens), tokens)

    def text_rows(owner):
        text = ctx_hbm.shape[0]
        return pl.ds(pl.multiple_of(owner * text, text), text)

    def head_columns(owner):
        return pl.ds(pl.multiple_of(owner * width, width), width)

    def weight_rows(owner):
        return pl.ds(pl.multiple_of(owner * depth, depth), depth)

    sources = {Q: q_hbm, K: k_hbm, V: v_hbm, CTX: ctx_hbm, CQ: cq_hbm}
    buffers = {Q: q_buf, K: k_buf, V: v_buf, CTX: ctx_buf, CQ: cq_buf}

    def piece(which, owner):
        if which == CTX:
            return sources[which]
        return sources[which].at[:, head_columns(owner)]

    def landing(which, owner):
        rows = text_rows(owner) if which == CTX else token_rows(owner)
        return buffers[which].at[rows]

    def seq_copy(which, offset):
        return pltpu.make_async_remote_copy(
            src_ref=piece(which, seq_peer(offset)),
            dst_ref=landing(which, seq),
            send_sem=seq_send.at[which, offset],
            recv_sem=seq_recv.at[which, offset],
            device_id={"seq": seq_peer(offset)},
            device_id_type=pl.DeviceIdType.MESH,
        )

    def text_start_here(way, hop):
        if way == 0:
            return (seq >= hop) & (seq + 1 < seq_size)
        return (seq + hop < seq_size) & (seq >= 1)

    def text_lands_here(way, hop):
        return seq >= hop + 1 if way == 0 else seq + 1 + hop < seq_size

    def text_copy(way, hop):
        owner = seq - hop if way == 0 else seq + hop
        peer = seq_peer(1 if way == 0 else seq_size - 1)
        rows = text_rows(owner)
        return pltpu.make_async_remote_copy(
            src_ref=ctx_hbm if hop == 0 else ctx_buf.at[rows],
            dst_ref=ctx_buf.at[rows],
            send_sem=text_send.at[way, hop],
            recv_sem=text_recv.at[way, hop],
            device_id={"seq": peer},
            device_id_type=pl.DeviceIdType.MESH,
        )

    def start_text(hop):
        for way in range(2):

            @pl.when(text_start_here(way, hop))
            def _():
                text_copy(way, hop).start()

    def wait_text(hop):
        for way in range(2):

            @pl.when(text_lands_here(way, hop))
            def _():
                text_copy(way, hop).wait_recv()

    weights = ((wk_hbm, wk_buf), (wv_hbm, wv_buf))

    def chip_copy(which, offset):
        shard, gathered = weights[which]
        return pltpu.make_async_remote_copy(
            src_ref=shard,
            dst_ref=gathered.at[weight_rows(prompt)],
            send_sem=chip_send.at[which, offset],
            recv_sem=chip_recv.at[which, offset],
            device_id={"prompt": chip_peer(offset)},
            device_id_type=pl.DeviceIdType.MESH,
        )

    def pair_copy(which, offset):
        shard, gathered = weights[which]
        rows = weight_rows(chip_source(offset))
        return pltpu.make_async_remote_copy(
            src_ref=shard if offset == 0 else gathered.at[rows],
            dst_ref=gathered.at[rows],
            send_sem=pair_send.at[which, offset],
            recv_sem=pair_recv.at[which, offset],
            device_id={"prompt": partner},
            device_id_type=pl.DeviceIdType.MESH,
        )

    def out_copy(offset):
        return pltpu.make_async_remote_copy(
            src_ref=out_buf.at[token_rows(seq_source(offset))],
            dst_ref=out_hbm.at[:, head_columns(seq)],
            send_sem=out_send.at[offset],
            recv_sem=out_recv.at[offset],
            device_id={"seq": seq_source(offset)},
            device_id_type=pl.DeviceIdType.MESH,
        )

    offsets = range(1, seq_size)

    def start_pieces(*group):
        for offset in offsets:
            for which in group:
                seq_copy(which, offset).start()

    groups = [[], [], [(K,), (V,), (Q, CQ)]]
    start_text(0)
    for group in groups[0]:
        start_pieces(*group)
    for which in range(2):
        for offset in range(1, chips):
            chip_copy(which, offset).start()
    local_copies = [
        pltpu.make_async_copy(
            piece(which, seq), landing(which, seq), local_sem.at[which]
        )
        for which in (Q, K, V, CTX, CQ)
    ] + [
        pltpu.make_async_copy(
            weights[which][0], weights[which][1].at[weight_rows(prompt)], local_sem.at[5 + which]
        )
        for which in range(2)
    ]
    for copy in local_copies:
        copy.start()
    for which in range(2):
        pair_copy(which, 0).start()
    for copy in local_copies:
        copy.wait()

    def head_attend(query, key, value, length):
        scores = lax.dot_general(
            query, key, (((1,), (1,)), ((), ())), preferred_element_type=jnp.float32
        )
        if length is not None:
            slot = lax.broadcasted_iota(jnp.int32, scores.shape, 1)
            scores = jnp.where(slot < length, scores, -jnp.inf)
        row_max = jnp.max(scores, axis=1, keepdims=True)
        exps = jnp.exp((scores - row_max) * scaling)
        totals = jnp.sum(exps, axis=1, keepdims=True)
        mixed = jnp.dot(exps.astype(jnp.bfloat16), value, preferred_element_type=jnp.float32)
        return (mixed / totals).astype(jnp.bfloat16)

    def forward(which):
        for offset in range(1, chips):
            chip_copy(which, offset).wait_recv()
            pair_copy(which, offset).start()

    hops = seq_size - 1
    for hop in range(hops):
        wait_text(hop)
        if hop + 1 < hops:
            start_text(hop + 1)
        for group in sum(groups[hop + 1 : hop + 2], []):
            start_pieces(*group)
        if hop == min(1, hops - 1):
            forward(0)
    for group in sum(groups[hops + 1 :], []):
        start_pieces(*group)

    def project(which, target):
        for offset in range(chips):
            pair_copy(which, offset).wait_recv()
        gathered = weights[which][1]
        tile = math.gcd(width, 256)

        def column_tile(index, carry):
            columns = pl.ds(pl.multiple_of(index * tile, tile), tile)
            target[:, columns] = jnp.dot(
                ctx_buf[...], gathered[:, columns], preferred_element_type=jnp.float32
            ).astype(jnp.bfloat16)
            return carry

        lax.fori_loop(0, width // tile, column_tile, 0)

    project(0, text_keys)
    forward(1)
    project(1, text_values)
    for which in (K, V):
        for offset in offsets:
            seq_copy(which, offset).wait_recv()
    length = length_ref[0]

    for offset in range(seq_size):
        if offset:
            seq_copy(Q, offset).wait_recv()
            seq_copy(CQ, offset).wait_recv()
        rows = token_rows(seq_source(offset))

        def head_block(head, carry):
            columns = pl.ds(pl.multiple_of(head * HD, HD), HD)
            alone = head_attend(q_buf[rows, columns], k_buf[:, columns], v_buf[:, columns], None)
            part = head_attend(
                cq_buf[rows, columns], text_keys[:, columns], text_values[:, columns], length
            )
            out_buf[rows, columns] = (
                alone.astype(jnp.float32) + part.astype(jnp.float32)
            ).astype(jnp.bfloat16)
            return carry

        lax.fori_loop(0, heads, head_block, 0)
        if offset:
            out_copy(offset).start()
    own = pltpu.make_async_copy(
        out_buf.at[token_rows(seq)], out_hbm.at[:, head_columns(seq)], local_sem.at[7]
    )
    own.start()

    for which in (Q, K, V, CQ):
        for offset in offsets:
            seq_copy(which, offset).wait_send()
    for hop in range(hops):
        for way in range(2):

            @pl.when(text_start_here(way, hop))
            def _():
                text_copy(way, hop).wait_send()

    for which in range(2):
        for offset in range(1, chips):
            chip_copy(which, offset).wait_send()
        for offset in range(chips):
            pair_copy(which, offset).wait_send()
    own.wait()
    for offset in offsets:
        out_copy(offset).wait()


def body(
    seq_size,
    prompt_size,
    queries,
    self_keys,
    self_values,
    cross_queries,
    context,
    key_weight,
    value_weight,
    lengths,
):
    tokens = queries.shape[1]
    full = tokens * seq_size
    width = key_weight.shape[1]
    model = context.shape[2]
    chips = prompt_size // CORES
    text_full = context.shape[1] * seq_size
    activations = pltpu.VMEM((full, width), jnp.bfloat16)
    texts = pltpu.VMEM((text_full, width), jnp.bfloat16)
    dma = pltpu.SemaphoreType.DMA
    attended = pl.pallas_call(
        functools.partial(kernel, seq_size, prompt_size),
        out_shape=jax.ShapeDtypeStruct(queries.shape[1:], jnp.bfloat16),
        in_specs=[pl.BlockSpec(memory_space=pltpu.SMEM)]
        + [pl.BlockSpec(memory_space=pl.ANY)] * 7,
        out_specs=pl.BlockSpec(memory_space=pl.ANY),
        scratch_shapes=[activations] * 4
        + [pltpu.VMEM((text_full, model), jnp.bfloat16)]
        + [pltpu.VMEM((model, width), jnp.bfloat16)] * 2
        + [texts] * 2
        + [activations]
        + [
            dma((8,)),
            dma((5, seq_size)),
            dma((5, seq_size)),
            dma((2, seq_size)),
            dma((2, seq_size)),
            dma((2, chips)),
            dma((2, chips)),
            dma((2, chips)),
            dma((2, chips)),
            dma((seq_size,)),
            dma((seq_size,)),
        ],
        compiler_params=pltpu.CompilerParams(
            collective_id=0, has_side_effects=True, vmem_limit_bytes=60 * 1024 * 1024
        ),
    )(
        lengths,
        queries[0],
        self_keys[0],
        self_values[0],
        cross_queries[0],
        context[0],
        key_weight,
        value_weight,
    )
    return attended[None]


def solution(mesh):
    in_specs = (
        P("prompt", "seq", None),
        P("prompt", "seq", None),
        P("prompt", "seq", None),
        P("prompt", "seq", None),
        P("prompt", "seq", None),
        P("prompt", "seq"),
        P("prompt", "seq"),
        P("prompt"),
    )
    out_specs = P("prompt", "seq", None)
    step = functools.partial(body, mesh.shape["seq"], mesh.shape["prompt"])
    return jax.shard_map(step, mesh=mesh, in_specs=in_specs, out_specs=out_specs, check_vma=False)
```

```python
import functools
import math

import jax
import jax.numpy as jnp
from jax import lax
from jax.experimental import pallas as pl
from jax.experimental.pallas import tpu as pltpu
from jax.sharding import PartitionSpec as P

HD = 128
CORES = 2
Q, K, V, CTX, CQ = range(5)


def kernel(
    seq_size,
    prompt_size,
    length_ref,
    q_hbm,
    k_hbm,
    v_hbm,
    cq_hbm,
    ctx_hbm,
    wk_hbm,
    wv_hbm,
    out_hbm,
    q_buf,
    k_buf,
    v_buf,
    cq_buf,
    ctx_buf,
    wk_buf,
    wv_buf,
    text_keys,
    text_values,
    self_buf,
    out_buf,
    local_sem,
    seq_send,
    seq_recv,
    text_send,
    text_recv,
    chip_send,
    chip_recv,
    pair_send,
    pair_recv,
    out_send,
    out_recv,
):
    seq = lax.axis_index("seq")
    prompt = lax.axis_index("prompt")
    chips = prompt_size // CORES
    chip = prompt // CORES
    core = prompt % CORES
    partner = chip * CORES + (1 - core)
    tokens = q_hbm.shape[0]
    width = wk_hbm.shape[1]
    depth = wk_hbm.shape[0]
    heads = width // HD
    scaling = 1.0 / math.sqrt(HD)

    def seq_peer(offset):
        return lax.rem(seq + offset, seq_size)

    def seq_source(offset):
        return lax.rem(seq + seq_size - offset, seq_size)

    def chip_peer(offset):
        return lax.rem(chip + offset, chips) * CORES + core

    def chip_source(offset):
        return lax.rem(chip + chips - offset, chips) * CORES + core

    barrier = pltpu.get_barrier_semaphore()
    for offset in range(1, seq_size):
        pl.semaphore_signal(
            barrier, inc=1, device_id={"seq": seq_peer(offset)}, device_id_type=pl.DeviceIdType.MESH
        )
    for offset in range(1, chips):
        pl.semaphore_signal(
            barrier,
            inc=1,
            device_id={"prompt": chip_peer(offset)},
            device_id_type=pl.DeviceIdType.MESH,
        )
    pl.semaphore_signal(
        barrier, inc=1, device_id={"prompt": partner}, device_id_type=pl.DeviceIdType.MESH
    )
    pl.semaphore_wait(barrier, seq_size - 1 + chips - 1 + 1)

    def token_rows(owner):
        return pl.ds(pl.multiple_of(owner * tokens, tokens), tokens)

    def text_rows(owner):
        text = ctx_hbm.shape[0]
        return pl.ds(pl.multiple_of(owner * text, text), text)

    def head_columns(owner):
        return pl.ds(pl.multiple_of(owner * width, width), width)

    def weight_rows(owner):
        return pl.ds(pl.multiple_of(owner * depth, depth), depth)

    sources = {Q: q_hbm, K: k_hbm, V: v_hbm, CTX: ctx_hbm, CQ: cq_hbm}
    buffers = {Q: q_buf, K: k_buf, V: v_buf, CTX: ctx_buf, CQ: cq_buf}

    def piece(which, owner):
        if which == CTX:
            return sources[which]
        return sources[which].at[:, head_columns(owner)]

    def landing(which, owner):
        rows = text_rows(owner) if which == CTX else token_rows(owner)
        return buffers[which].at[rows]

    def seq_copy(which, offset):
        return pltpu.make_async_remote_copy(
            src_ref=piece(which, seq_peer(offset)),
            dst_ref=landing(which, seq),
            send_sem=seq_send.at[which, offset],
            recv_sem=seq_recv.at[which, offset],
            device_id={"seq": seq_peer(offset)},
            device_id_type=pl.DeviceIdType.MESH,
        )

    def text_start_here(way, hop):
        if way == 0:
            return (seq >= hop) & (seq + 1 < seq_size)
        return (seq + hop < seq_size) & (seq >= 1)

    def text_lands_here(way, hop):
        return seq >= hop + 1 if way == 0 else seq + 1 + hop < seq_size

    def text_copy(way, hop):
        owner = seq - hop if way == 0 else seq + hop
        peer = seq_peer(1 if way == 0 else seq_size - 1)
        rows = text_rows(owner)
        return pltpu.make_async_remote_copy(
            src_ref=ctx_hbm if hop == 0 else ctx_buf.at[rows],
            dst_ref=ctx_buf.at[rows],
            send_sem=text_send.at[way, hop],
            recv_sem=text_recv.at[way, hop],
            device_id={"seq": peer},
            device_id_type=pl.DeviceIdType.MESH,
        )

    def start_text(hop):
        for way in range(2):

            @pl.when(text_start_here(way, hop))
            def _():
                text_copy(way, hop).start()

    def wait_text(hop):
        for way in range(2):

            @pl.when(text_lands_here(way, hop))
            def _():
                text_copy(way, hop).wait_recv()

    weights = ((wk_hbm, wk_buf), (wv_hbm, wv_buf))

    def chip_copy(which, offset):
        shard, gathered = weights[which]
        return pltpu.make_async_remote_copy(
            src_ref=shard,
            dst_ref=gathered.at[weight_rows(prompt)],
            send_sem=chip_send.at[which, offset],
            recv_sem=chip_recv.at[which, offset],
            device_id={"prompt": chip_peer(offset)},
            device_id_type=pl.DeviceIdType.MESH,
        )

    def pair_copy(which, offset):
        shard, gathered = weights[which]
        rows = weight_rows(chip_source(offset))
        return pltpu.make_async_remote_copy(
            src_ref=shard if offset == 0 else gathered.at[rows],
            dst_ref=gathered.at[rows],
            send_sem=pair_send.at[which, offset],
            recv_sem=pair_recv.at[which, offset],
            device_id={"prompt": partner},
            device_id_type=pl.DeviceIdType.MESH,
        )

    def out_copy(offset):
        return pltpu.make_async_remote_copy(
            src_ref=out_buf.at[token_rows(seq_source(offset))],
            dst_ref=out_hbm.at[:, head_columns(seq)],
            send_sem=out_send.at[offset],
            recv_sem=out_recv.at[offset],
            device_id={"seq": seq_source(offset)},
            device_id_type=pl.DeviceIdType.MESH,
        )

    offsets = range(1, seq_size)

    def start_pieces(*group):
        for offset in sorted(offsets, key=lambda offset: abs(2 * offset - seq_size)):
            for which in group:
                seq_copy(which, offset).start()

    groups = [[], [], [(K,), (V,), (Q,), (CQ,)]]
    start_text(0)
    for group in groups[0]:
        start_pieces(*group)
    for which in range(2):
        for offset in range(1, chips):
            chip_copy(which, offset).start()
    local_copies = [
        pltpu.make_async_copy(
            piece(which, seq), landing(which, seq), local_sem.at[which]
        )
        for which in (Q, K, V, CTX, CQ)
    ] + [
        pltpu.make_async_copy(
            weights[which][0], weights[which][1].at[weight_rows(prompt)], local_sem.at[5 + which]
        )
        for which in range(2)
    ]
    for copy in local_copies:
        copy.start()
    for which in range(2):
        pair_copy(which, 0).start()
    for copy in local_copies:
        copy.wait()

    def head_attend(query, key, value, length):
        scores = lax.dot_general(
            query, key, (((1,), (1,)), ((), ())), preferred_element_type=jnp.float32
        )
        if length is not None:
            slot = lax.broadcasted_iota(jnp.int32, scores.shape, 1)
            scores = jnp.where(slot < length, scores, -jnp.inf)
        row_max = jnp.max(scores, axis=1, keepdims=True)
        exps = jnp.exp((scores - row_max) * scaling)
        totals = jnp.sum(exps, axis=1, keepdims=True)
        mixed = jnp.dot(exps.astype(jnp.bfloat16), value, preferred_element_type=jnp.float32)
        return (mixed / totals).astype(jnp.bfloat16)

    def forward(which):
        for offset in range(1, chips):
            chip_copy(which, offset).wait_recv()
            pair_copy(which, offset).start()

    hops = seq_size - 1
    for hop in range(hops):
        wait_text(hop)
        if hop + 1 < hops:
            start_text(hop + 1)
        for group in sum(groups[hop + 1 : hop + 2], []):
            start_pieces(*group)
        if hop == min(1, hops - 1):
            forward(0)
    for group in sum(groups[hops + 1 :], []):
        start_pieces(*group)

    def project(which, target):
        for offset in range(chips):
            pair_copy(which, offset).wait_recv()
        gathered = weights[which][1]
        tile = math.gcd(width, 256)

        def column_tile(index, carry):
            columns = pl.ds(pl.multiple_of(index * tile, tile), tile)
            target[:, columns] = jnp.dot(
                ctx_buf[...], gathered[:, columns], preferred_element_type=jnp.float32
            ).astype(jnp.bfloat16)
            return carry

        lax.fori_loop(0, width // tile, column_tile, 0)

    project(0, text_keys)
    forward(1)
    project(1, text_values)
    for which in (K, V, Q):
        for offset in offsets:
            seq_copy(which, offset).wait_recv()

    def self_head(head, carry):
        columns = pl.ds(pl.multiple_of(head * HD, HD), HD)
        key = k_buf[:, columns]
        value = v_buf[:, columns]

        def block(index, inner):
            rows = token_rows(index)
            self_buf[rows, columns] = head_attend(q_buf[rows, columns], key, value, None)
            return inner

        return lax.fori_loop(0, seq_size, block, carry)

    lax.fori_loop(0, heads, self_head, 0)
    length = length_ref[0]

    arrival = sorted(offsets, key=lambda offset: abs(2 * offset - seq_size))
    for offset in arrival + [0]:
        if offset:
            seq_copy(CQ, offset).wait_recv()
        rows = token_rows(seq_source(offset))

        def head_block(head, carry):
            columns = pl.ds(pl.multiple_of(head * HD, HD), HD)
            alone = self_buf[rows, columns]
            part = head_attend(
                cq_buf[rows, columns], text_keys[:, columns], text_values[:, columns], length
            )
            out_buf[rows, columns] = (
                alone.astype(jnp.float32) + part.astype(jnp.float32)
            ).astype(jnp.bfloat16)
            return carry

        lax.fori_loop(0, heads, head_block, 0)
        if offset:
            out_copy(offset).start()
    own = pltpu.make_async_copy(
        out_buf.at[token_rows(seq)], out_hbm.at[:, head_columns(seq)], local_sem.at[7]
    )
    own.start()

    for which in (Q, K, V, CQ):
        for offset in offsets:
            seq_copy(which, offset).wait_send()
    for hop in range(hops):
        for way in range(2):

            @pl.when(text_start_here(way, hop))
            def _():
                text_copy(way, hop).wait_send()

    for which in range(2):
        for offset in range(1, chips):
            chip_copy(which, offset).wait_send()
        for offset in range(chips):
            pair_copy(which, offset).wait_send()
    own.wait()
    for offset in offsets:
        out_copy(offset).wait()


def body(
    seq_size,
    prompt_size,
    queries,
    self_keys,
    self_values,
    cross_queries,
    context,
    key_weight,
    value_weight,
    lengths,
):
    tokens = queries.shape[1]
    full = tokens * seq_size
    width = key_weight.shape[1]
    model = context.shape[2]
    chips = prompt_size // CORES
    text_full = context.shape[1] * seq_size
    activations = pltpu.VMEM((full, width), jnp.bfloat16)
    texts = pltpu.VMEM((text_full, width), jnp.bfloat16)
    dma = pltpu.SemaphoreType.DMA
    attended = pl.pallas_call(
        functools.partial(kernel, seq_size, prompt_size),
        out_shape=jax.ShapeDtypeStruct(queries.shape[1:], jnp.bfloat16),
        in_specs=[pl.BlockSpec(memory_space=pltpu.SMEM)]
        + [pl.BlockSpec(memory_space=pl.ANY)] * 7,
        out_specs=pl.BlockSpec(memory_space=pl.ANY),
        scratch_shapes=[activations] * 4
        + [pltpu.VMEM((text_full, model), jnp.bfloat16)]
        + [pltpu.VMEM((model, width), jnp.bfloat16)] * 2
        + [texts] * 2
        + [activations] * 2
        + [
            dma((8,)),
            dma((5, seq_size)),
            dma((5, seq_size)),
            dma((2, seq_size)),
            dma((2, seq_size)),
            dma((2, chips)),
            dma((2, chips)),
            dma((2, chips)),
            dma((2, chips)),
            dma((seq_size,)),
            dma((seq_size,)),
        ],
        compiler_params=pltpu.CompilerParams(
            collective_id=0, has_side_effects=True, vmem_limit_bytes=60 * 1024 * 1024
        ),
    )(
        lengths,
        queries[0],
        self_keys[0],
        self_values[0],
        cross_queries[0],
        context[0],
        key_weight,
        value_weight,
    )
    return attended[None]


def solution(mesh):
    in_specs = (
        P("prompt", "seq", None),
        P("prompt", "seq", None),
        P("prompt", "seq", None),
        P("prompt", "seq", None),
        P("prompt", "seq", None),
        P("prompt", "seq"),
        P("prompt", "seq"),
        P("prompt"),
    )
    out_specs = P("prompt", "seq", None)
    step = functools.partial(body, mesh.shape["seq"], mesh.shape["prompt"])
    return jax.shard_map(step, mesh=mesh, in_specs=in_specs, out_specs=out_specs, check_vma=False)
```
